32 devices in a mesh: segment: 4 (over z), expert: 2 (over y), dp: 4 (over x, core).
Axes of the slice: x: 2, y: 2, z: 4, core: 2. Of those that a mesh axis runs over, the one named last changes fastest.
Arguments:
- state_in: bfloat16 [4, 4, 1024, 2048], P('segment', None, ('expert', 'dp')), may hold values from -6 to 6
- entering: bfloat16 [1, 4, 1024, 2048], P(None, None, ('expert', 'dp')), may hold values from -6 to 6
- saved: bfloat16 [4, 2, 2, 1024, 2048], P('segment', None, None, ('expert', 'dp')), may hold values from -6 to 6
- route_ids: int32 [4, 2, 4, 2, 1024, 6], P('segment', None, None, None, ('expert', 'dp')), may hold values from 0 to 63, as said below
- gate_vals: float32 [4, 2, 4, 2, 1024, 6], P('segment', None, None, None, ('expert', 'dp')), may hold values from 0.25 to 1
- w_gate: bfloat16 [4, 2, 2048, 1408], P('segment', 'expert', None, 'dp'), may hold values from -0.125 to 0.125
- w_up: bfloat16 [4, 2, 2048, 1408], P('segment', 'expert', None, 'dp'), may hold values from -0.125 to 0.125
- w_down: bfloat16 [4, 2, 1408, 2048], P('segment', 'expert', 'dp'), may hold values from -0.15625 to 0.15625
- gains: float32 [4, 2, 2048], P('segment'), may hold values from 0.5 to 2
Outputs:
- state_out: bfloat16 [4, 4, 1024, 2048], P('segment', None, ('expert', 'dp'))
The draws below stay inside these ranges and needn't reach their ends.
Inputs may be any that keep to these rules, and one draw needn't show every extreme that they name: `route_ids`: the ids of one token are distinct, and a token names at most one id under 1. Within each block of 128 consecutive tokens (the tokens of one device) an id under 1 is named by at most 8 tokens. For every section, slot, unit and sublayer some id under 1 is named by exactly 8 tokens in every block, and every block has an id under 1 named by exactly 8 of its tokens.
All inputs are finite; a program needn't handle non-finite values.
Results may differ from the reference program's by a relative error of at most 0.017.
Values may be sent and summed in bfloat16 or wider, within the bound.
A program may use at most 128 MiB of HBM per device.

```python
import math
import jax
import jax.numpy as jnp
from jax import lax

D = 2048
FF = 1408
ROUTED = 64
TOPK = 6
TOK = 128
CAP = 8
SLOTS = 2
EXPERTS = 1
FFQ = 352
TOKENS = 1024
SEGMENTS = 4
N_DP = 4


def draw_route_ids(key, part):
    leading = SEGMENTS * SLOTS * 4 * 2
    blocks = TOKENS // TOK
    subkeys = jax.random.split(jax.random.fold_in(key, 11), 6)
    counts = jax.random.randint(subkeys[0], (leading, blocks, EXPERTS), 0, CAP + 1)
    busiest = jax.random.randint(subkeys[1], (leading, 1, 1), 0, EXPERTS)
    second = jax.random.randint(subkeys[2], (leading, blocks, 1), 0, EXPERTS)
    experts = jnp.arange(EXPERTS, dtype=jnp.int32)
    counts = jnp.where((experts[None, None, :] == busiest) | (experts[None, None, :] == second), CAP, counts)
    starts = jnp.cumsum(counts, axis=-1) - counts
    order_keys = jax.random.split(subkeys[3], leading * blocks)
    places = jax.vmap(lambda subkey: jax.random.permutation(subkey, TOK))(order_keys).reshape(leading, blocks, TOK)
    inside = (places[:, :, :, None] >= starts[:, :, None, :]) & (places[:, :, :, None] < (starts + counts)[:, :, None, :])
    has_route = jnp.sum(inside.astype(jnp.int32), axis=-1)
    chosen = jnp.sum(jnp.where(inside, experts, 0), axis=-1)
    others = ROUTED - EXPERTS
    scores = jax.random.randint(subkeys[4], (leading, blocks, TOK, others), 0, 1 << 20) * others + jnp.arange(others, dtype=jnp.int32)
    ignored, picked = lax.top_k(scores, TOPK)
    filler = picked.astype(jnp.int32) + EXPERTS
    column = jax.random.randint(subkeys[5], (leading, blocks, TOK, 1), 0, TOPK)
    positions = jnp.arange(TOPK, dtype=jnp.int32)
    route_ids = jnp.where((has_route[..., None] == 1) & (positions == column), chosen[..., None], filler)
    return route_ids.reshape(SEGMENTS, SLOTS, 4, 2, TOKENS, TOPK)


def shard_levels(key, dims, cuts, smallest, top_value):
    def one(position, parts):
        heights = jax.random.uniform(jax.random.fold_in(jax.random.fold_in(key, 6), position), (parts,), jnp.float32, smallest / len(cuts), top_value / len(cuts))
        return jnp.repeat(jnp.exp(heights), dims[position] // parts).reshape((-1,) + (1,) * (len(dims) - position - 1))

    loudness = one(*cuts[0])
    for cut in cuts[1:]:
        loudness = loudness * one(*cut)
    return loudness


def noise(key, extent, width, limit, cuts=(), held_as=jnp.bfloat16):
    level = shard_levels(key, extent, cuts, -0.22, 0.18) if cuts else 1.0
    values = jax.random.normal(key, extent, jnp.float32) * width * level
    return jnp.minimum(jnp.maximum(values, -limit), limit).astype(held_as)


def setup_inputs(seed: int = 0) -> dict:
    arg_keys = jax.random.split(jax.random.key(seed), 10)
    return {
        "state_in": noise(arg_keys[0], (SEGMENTS, 4, TOKENS, D), 1.0, 6.0, ((0, 4), (2, 8))),
        "entering": noise(arg_keys[1], (SLOTS - 1, 4, TOKENS, D), 1.0, 6.0, ((2, 8),)),
        "saved": noise(arg_keys[2], (SEGMENTS, SLOTS, 2, TOKENS, D), 1.0, 6.0, ((0, 4), (3, 8))),
        "route_ids": draw_route_ids(jax.random.fold_in(arg_keys[9], 71), 0),
        "gate_vals": jnp.clip(0.25 + 0.75 * jax.random.uniform(arg_keys[4], (SEGMENTS, SLOTS, 4, 2, TOKENS, TOPK), jnp.float32) ** shard_levels(arg_keys[4], (SEGMENTS, SLOTS, 4, 2, TOKENS, TOPK), ((0, 4), (4, 8)), -0.2, 0.2), 0.25, 1.0),
        "w_gate": noise(arg_keys[5], (SEGMENTS, 2 * EXPERTS, D, FF), D ** -0.5, 0.125, ((0, 4), (1, 2), (3, 4))),
        "w_up": noise(arg_keys[6], (SEGMENTS, 2 * EXPERTS, D, FF), D ** -0.5, 0.125, ((0, 4), (1, 2), (3, 4))),
        "w_down": noise(arg_keys[7], (SEGMENTS, 2 * EXPERTS, FF, D), FF ** -0.5, 0.15625, ((0, 4), (1, 2), (2, 4))),
        "gains": jnp.clip(jnp.exp(math.log(2.0) - 1.3862944 * jax.random.uniform(arg_keys[8], (SEGMENTS, 2, D), jnp.float32) ** shard_levels(arg_keys[8], (SEGMENTS, 2, D), ((0, 4),), -0.2, 0.2)), 0.5, 2.0),
    }


EPSILON = 1e-06
HIGHEST = lax.Precision.HIGHEST
CONTRACT_LAST = (((1,), (1,)), ((), ()))

def route_tables(block_ids, block_gates):
    expert_range = jnp.arange(EXPERTS, dtype=jnp.int32)
    matches = block_ids[:, :, None] == expert_range[None, None, :]
    routed = lax.optimization_barrier(jnp.sum(matches.astype(jnp.int32), axis=1))
    weighting = lax.optimization_barrier(jnp.sum(jnp.where(matches, block_gates[:, :, None], jnp.zeros_like(block_gates[:, :, None])), axis=1))
    earlier = jnp.cumsum(routed, axis=0) - routed
    slot_range = jnp.arange(CAP, dtype=jnp.int32)
    chosen = (routed[:, :, None] == 1) & (earlier[:, :, None] == slot_range[None, None, :])
    row_total = block_ids.shape[0]
    selector = jnp.transpose(chosen.reshape(row_total, EXPERTS * CAP)).astype(block_gates.dtype)
    slot_gate = lax.optimization_barrier(jnp.sum(jnp.where(chosen, weighting[:, :, None], jnp.zeros_like(weighting[:, :, None])), axis=0))
    return (selector, slot_gate.reshape(EXPERTS * CAP))

def tables_of(unit_ids, unit_gates):
    blocks = TOKENS // TOK
    return jax.vmap(route_tables)(unit_ids.reshape(blocks, TOK, TOPK), unit_gates.reshape(blocks, TOK, TOPK))

def norm_rows(values, norm_gain):
    inverse_rms = lax.rsqrt(lax.optimization_barrier(jnp.mean(values * values, axis=-1, keepdims=True)) + EPSILON)
    return ((values * inverse_rms * norm_gain).astype(jnp.bfloat16), inverse_rms)

def norm_back(values, inverse_rms, norm_gain, delta, grad_normed):
    weighted = norm_gain * grad_normed
    cubed = inverse_rms * inverse_rms * inverse_rms
    return delta + inverse_rms * weighted - values * cubed * lax.optimization_barrier(jnp.sum(weighted * values, axis=-1, keepdims=True)) / values.shape[-1]

def select_rows(selector, values):
    blocks = TOKENS // TOK
    return jnp.einsum('bst,btd->bsd', selector, values.reshape(blocks, TOK, D).astype(selector.dtype), precision=HIGHEST)

def spread_rows(selector, slot_values):
    return jnp.einsum('bst,bsd->btd', selector, slot_values, precision=HIGHEST).reshape(TOKENS, D)

def expert_slice(slot_rows, expert_index):
    blocks = TOKENS // TOK
    return slot_rows.reshape(blocks, EXPERTS, CAP, D)[:, expert_index].reshape(blocks * CAP, D)

def expert_forward(hidden_rows, gate_weight, up_weight):
    gate_pre = jnp.dot(hidden_rows, gate_weight, preferred_element_type=jnp.float32)
    up_pre = jnp.dot(hidden_rows, up_weight, preferred_element_type=jnp.float32)
    return (gate_pre, up_pre)

def expert_back(grad_in_rows, gate_pre, up_pre, gate_weight, up_weight, down_weight):
    grad_act = lax.dot_general(grad_in_rows, down_weight, CONTRACT_LAST, preferred_element_type=jnp.float32)
    sigmoid_gate = jax.nn.sigmoid(gate_pre)
    grad_gate = (grad_act * up_pre * sigmoid_gate * (1.0 + gate_pre * (1.0 - sigmoid_gate))).astype(jnp.bfloat16)
    grad_up = (grad_act * gate_pre * sigmoid_gate).astype(jnp.bfloat16)
    grad_hidden = lax.dot_general(grad_gate, gate_weight, CONTRACT_LAST, preferred_element_type=jnp.float32)
    grad_hidden = grad_hidden + lax.dot_general(grad_up, up_weight, CONTRACT_LAST, preferred_element_type=jnp.float32)
    return grad_hidden.astype(jnp.bfloat16)

def sublayer(values, unit_ids, unit_gates, layer):
    gate_all, up_all, down_all, norm_gain = layer
    blocks = TOKENS // TOK
    selector, slot_gate = tables_of(unit_ids, unit_gates)
    normed, inverse_rms = norm_rows(values, norm_gain)
    slot_rows = select_rows(selector, normed).astype(jnp.bfloat16)
    outputs = []
    for expert_index in range(EXPERTS):
        hidden_rows = expert_slice(slot_rows, expert_index)
        gate_pre, up_pre = expert_forward(hidden_rows, gate_all[expert_index], up_all[expert_index])
        activation = (jax.nn.silu(gate_pre) * up_pre).astype(jnp.bfloat16)
        summed = jnp.zeros((hidden_rows.shape[0], D), jnp.float32)
        for quarter in range(N_DP):
            offset = quarter * FFQ
            partial_value = jnp.dot(activation[:, offset:offset + FFQ], down_all[expert_index, offset:offset + FFQ], preferred_element_type=jnp.float32).astype(jnp.bfloat16)
            summed = summed + lax.optimization_barrier(partial_value).astype(jnp.float32)
        outputs.append(summed.reshape(blocks, CAP, D))
    expert_out = jnp.stack(outputs, axis=1).reshape(blocks, EXPERTS * CAP, D)
    return values + spread_rows(selector, slot_gate[:, :, None] * expert_out)

def sublayer_back(values, delta, unit_ids, unit_gates, layer):
    gate_all, up_all, down_all, norm_gain = layer
    blocks = TOKENS // TOK
    selector, slot_gate = tables_of(unit_ids, unit_gates)
    normed, inverse_rms = norm_rows(values, norm_gain)
    slot_rows = select_rows(selector, normed).astype(jnp.bfloat16)
    slot_grads = (slot_gate[:, :, None] * select_rows(selector, delta)).astype(jnp.bfloat16)
    outputs = []
    for expert_index in range(EXPERTS):
        hidden_rows = expert_slice(slot_rows, expert_index)
        grad_in_rows = expert_slice(slot_grads, expert_index)
        gate_pre, up_pre = expert_forward(hidden_rows, gate_all[expert_index], up_all[expert_index])
        summed = jnp.zeros((hidden_rows.shape[0], D), jnp.float32)
        for quarter in range(N_DP):
            offset = quarter * FFQ
            partial_value = expert_back(grad_in_rows, gate_pre[:, offset:offset + FFQ], up_pre[:, offset:offset + FFQ], gate_all[expert_index][:, offset:offset + FFQ], up_all[expert_index][:, offset:offset + FFQ], down_all[expert_index, offset:offset + FFQ])
            summed = summed + lax.optimization_barrier(partial_value).astype(jnp.float32)
        outputs.append(summed.reshape(blocks, CAP, D))
    grad_normed = spread_rows(selector, jnp.stack(outputs, axis=1).reshape(blocks, EXPERTS * CAP, D))
    return norm_back(values, inverse_rms, norm_gain, delta, grad_normed)

def forward_unit(start, unit_ids, unit_gates, layers, order):
    values = start.astype(jnp.float32)
    for sub_index in order:
        values = sublayer(values, unit_ids[sub_index], unit_gates[sub_index], layers[sub_index])
    return values.astype(jnp.bfloat16)

def backward_unit(kept, incoming, unit_ids, unit_gates, layers, order):
    first_sub = order[0]
    second_sub = order[1]
    start = kept.astype(jnp.float32)
    middle = sublayer(start, unit_ids[first_sub], unit_gates[first_sub], layers[first_sub])
    grad_middle = sublayer_back(middle, incoming.astype(jnp.float32), unit_ids[second_sub], unit_gates[second_sub], layers[second_sub])
    grad_start = sublayer_back(start, grad_middle, unit_ids[first_sub], unit_gates[first_sub], layers[first_sub])
    return grad_start.astype(jnp.bfloat16)

def reference(state_in, entering, saved, route_ids, gate_vals, w_gate, w_up, w_down, gains):
    current = state_in
    result = state_in
    for slot_index in range(SLOTS):
        produced = []
        for segment_index in range(SEGMENTS):
            layers = [(w_gate[segment_index, sub_index * EXPERTS:(sub_index + 1) * EXPERTS], w_up[segment_index, sub_index * EXPERTS:(sub_index + 1) * EXPERTS], w_down[segment_index, sub_index * EXPERTS:(sub_index + 1) * EXPERTS], gains[segment_index, sub_index]) for sub_index in range(2)]
            ids_here = route_ids[segment_index, slot_index]
            gates_here = gate_vals[segment_index, slot_index]
            first_forward = forward_unit(current[segment_index, 0], ids_here[0], gates_here[0], layers, (0, 1))
            second_forward = forward_unit(current[segment_index, 1], ids_here[1], gates_here[1], layers, (1, 0))
            first_backward = backward_unit(saved[segment_index, slot_index, 0], current[segment_index, 2], ids_here[2], gates_here[2], layers, (0, 1))
            second_backward = backward_unit(saved[segment_index, slot_index, 1], current[segment_index, 3], ids_here[3], gates_here[3], layers, (1, 0))
            produced.append(jnp.stack([first_forward, second_forward, first_backward, second_backward]))
        result = jnp.stack(produced)
        if slot_index + 1 < SLOTS:
            arriving = entering[slot_index]
            acts_up = jnp.concatenate([arriving[0][None], result[:-1, 0]], axis=0)
            acts_down = jnp.concatenate([result[1:, 1], arriving[1][None]], axis=0)
            grads_down = jnp.concatenate([result[1:, 2], arriving[2][None]], axis=0)
            grads_up = jnp.concatenate([arriving[3][None], result[:-1, 3]], axis=0)
            current = jnp.stack([acts_up, acts_down, grads_down, grads_up], axis=1)
    return result
```

```python
import functools
import jax
import jax.numpy as jnp
from jax import lax
from jax.experimental import pallas as pl
from jax.experimental.pallas import tpu as pltpu
from jax.sharding import PartitionSpec as P

CAP = 8
EPSILON = 1e-06
LAST = (((1,), (1,)), ((), ()))
MESH = pl.DeviceIdType.MESH
BF = jnp.bfloat16
F32 = jnp.float32
ITEMS_OUT = (3, 4, 2, 2, 1)
ITEMS_BACK = (3, 2, 2, 2, 1)


def mm(a, b):
    return jnp.dot(a, b, preferred_element_type=F32)


def mm_t(a, b):
    return lax.dot_general(a, b, LAST, preferred_element_type=F32)


def mix(overlap, rows):
    return jnp.dot(overlap, rows, preferred_element_type=F32, precision=lax.Precision.HIGHEST)


def unit_norm(rows, gain):
    inv = lax.rsqrt(jnp.mean(rows * rows, axis=-1, keepdims=True) + EPSILON)
    return (rows * inv * gain).astype(BF), inv


def back_norm(rows, inv, gain, grad):
    weighted = gain * grad
    total = jnp.sum(weighted * rows, axis=-1, keepdims=True)
    return inv * weighted - rows * (inv * inv * inv) * total / rows.shape[-1]


def kernel(sizes, state, entering, saved, ids, gates, wg_in, wu_in, wd_in, gains, out, *scratch):
    ns, ne, nd = sizes
    group = ne * nd
    ec = ne // 2
    width = ec * CAP
    tokens, model = state.shape[1], state.shape[2]
    outs, ins, back_outs, back_ins = scratch[0:5], scratch[5:10], scratch[10:15], scratch[15:20]
    (base, patch_out, patch_in, sel, gate_col, vals, pre, wg, wu, wd,
     send_sem, recv_sem, local_sem, relay_send, relay_recv, enter_sem, weight_sem) = scratch[20:]
    seg, ex, dp = lax.axis_index("segment"), lax.axis_index("expert"), lax.axis_index("dp")
    me = ex * nd + dp

    weight_copies = [
        pltpu.make_async_copy(source, dest, weight_sem.at[i])
        for i, (source, dest) in enumerate(((wg_in, wg), (wu_in, wu), (wd_in, wd)))
    ]
    for copy in weight_copies:
        copy.start()

    barrier = pltpu.get_barrier_semaphore()

    @pl.loop(1, group)
    def _(k):
        t = lax.rem(me + k, group)
        pl.semaphore_signal(
            barrier, inc=1, device_id=(seg, lax.div(t, nd), lax.rem(t, nd)), device_id_type=MESH
        )

    has_up, has_down = seg < ns - 1, seg > 0

    @pl.when(has_up)
    def _():
        pl.semaphore_signal(barrier, inc=1, device_id=(seg + 1, ex, dp), device_id_type=MESH)

    @pl.when(has_down)
    def _():
        pl.semaphore_signal(barrier, inc=1, device_id=(seg - 1, ex, dp), device_id_type=MESH)

    neighbours = jnp.where(has_up, 1, 0) + jnp.where(has_down, 1, 0)
    pl.semaphore_wait(barrier, group - 1 + neighbours)

    def relay(unit, kind, source, dest):
        up = unit in (0, 3)
        goes, comes = (has_up, has_down) if up else (has_down, has_up)
        target = lax.rem(seg + (1 if up else ns - 1), ns)
        copy = pltpu.make_async_remote_copy(
            src_ref=source, dst_ref=dest, send_sem=relay_send.at[kind, unit],
            recv_sem=relay_recv.at[kind, unit], device_id=(target, ex, dp), device_id_type=MESH,
        )
        return goes, comes, copy

    def start_if(triple):
        @pl.when(triple[0])
        def _():
            triple[2].start()

    bulk = [relay(u, 0, state.at[u], base.at[u]) for u in range(4)]
    enter = [pltpu.make_async_copy(entering.at[u], base.at[u], enter_sem.at[u]) for u in range(4)]
    for u in range(4):
        start_if(bulk[u])

        @pl.when(jnp.logical_not(bulk[u][1]))
        def _(u=u):
            enter[u].start()

    def wait_bulk(u):
        @pl.when(bulk[u][1])
        def _():
            bulk[u][2].wait_recv()

        @pl.when(jnp.logical_not(bulk[u][1]))
        def _():
            enter[u].wait()

    patches = [relay(u, 1, patch_out.at[u], patch_in.at[u]) for u in range(4)]
    for u in range(4):
        @pl.when(jnp.logical_not(patches[u][1]))
        def _(u=u):
            patch_in[u] = jnp.zeros(patch_in.shape[1:], BF)

    def wait_patch(u):
        @pl.when(patches[u][1])
        def _():
            patches[u][2].wait_recv()

    def peer(t):
        return (seg, lax.div(t, nd), lax.rem(t, nd))

    def step_copy(r, k, outward, target):
        if outward:
            source, dest, phase = outs[r].at[lax.div(target, nd)], ins[r].at[me], 2 * r
        else:
            source, dest, phase = back_outs[r].at[target], back_ins[r].at[me], 2 * r + 1
        return pltpu.make_async_remote_copy(
            src_ref=source, dst_ref=dest, send_sem=send_sem.at[phase, k],
            recv_sem=recv_sem.at[phase, k], device_id=peer(target), device_id_type=MESH,
        )

    def own_copy(r, outward):
        if outward:
            return pltpu.make_async_copy(outs[r].at[ex], ins[r].at[me], local_sem.at[2 * r])
        return pltpu.make_async_copy(back_outs[r].at[me], back_ins[r].at[me], local_sem.at[2 * r + 1])

    def send(r, outward):
        @pl.loop(1, group)
        def _(k):
            step_copy(r, k, outward, lax.rem(me + k, group)).start()

        own_copy(r, outward).start()

    def receive(r, outward):
        phase = 2 * r if outward else 2 * r + 1
        arrived = ins[r] if outward else back_ins[r]

        @pl.loop(1, group)
        def _(k):
            slot = arrived.at[lax.rem(me - k + group, group)]
            pltpu.make_async_remote_copy(
                src_ref=slot, dst_ref=slot, send_sem=send_sem.at[phase, k],
                recv_sem=recv_sem.at[phase, k], device_id=peer(me), device_id_type=MESH,
            ).wait_recv()

        own_copy(r, outward).wait()

    def drain(r, outward):
        @pl.loop(1, group)
        def _(k):
            step_copy(r, k, outward, lax.rem(me + k, group)).wait_send()

    lane = lax.broadcasted_iota(jnp.int32, (tokens, tokens), 1)
    row = lax.broadcasted_iota(jnp.int32, (tokens, tokens), 0)
    before = (row < lane).astype(F32).astype(BF)
    eye = (row == lane).astype(F32)
    slot_row = lax.broadcasted_iota(jnp.int32, (CAP, tokens), 0).astype(F32)
    for e in range(ec):
        match = ids[...] == e
        routed = jnp.sum(match.astype(F32), axis=1)
        weight = jnp.sum(jnp.where(match, gates[...], 0.0), axis=1)
        earlier = mm(routed.astype(BF), before)
        for tb in range(ids.shape[0]):
            hit = (routed[tb:tb + 1] == 1.0) & (earlier[tb:tb + 1] == slot_row)
            one = jnp.where(hit, 1.0, 0.0)
            sel[tb, e * CAP:(e + 1) * CAP] = one
            gate_col[tb, e * CAP:(e + 1) * CAP] = jnp.broadcast_to(
                jnp.sum(one * weight[tb:tb + 1], axis=1, keepdims=True), (CAP, tokens)
            )

    def tab(slot, unit, sub):
        return (slot * 4 + unit) * 2 + sub

    def pick(slot, unit, values):
        first = unit % 2
        both = jnp.concatenate([sel[tab(slot, unit, first)], sel[tab(slot, unit, 1 - first)]])
        return mm(both.astype(BF), values)

    def pick_new(unit, old):
        first = unit % 2
        both = jnp.concatenate([sel[tab(1, unit, first)], sel[tab(1, unit, 1 - first)]])
        held = old[:, model:]
        keep = 1.0 - jnp.sum(held.astype(F32), axis=0, keepdims=True)
        moved = mm_t(both.astype(BF), held).astype(BF)
        return mm((both * keep).astype(BF), base[unit]) + mm(moved, old[:, :model])

    def overlap(slot, unit):
        first = unit % 2
        return mm_t(sel[tab(slot, unit, 1 - first)].astype(BF), sel[tab(slot, unit, first)].astype(BF))

    def overlap_t(slot, unit):
        first = unit % 2
        return mm_t(sel[tab(slot, unit, first)].astype(BF), sel[tab(slot, unit, 1 - first)].astype(BF))

    def gate(slot, unit, second):
        sub = 1 - unit % 2 if second else unit % 2
        return gate_col[tab(slot, unit, sub)][:, 0:1]

    def gain(unit, second):
        sub = 1 - unit % 2 if second else unit % 2
        return gains[sub:sub + 1]

    def put(r, item, unit, second, rows):
        side = 1 - unit % 2 if second else unit % 2
        for e in range(ec):
            outs[r][side * ec + e, item] = rows[e * CAP:(e + 1) * CAP].astype(BF)

    def got(r, item, unit, second):
        side = 1 - unit % 2 if second else unit % 2
        parts = []
        for e in range(ec):
            first = (side * ec + e) * nd
            total = back_ins[r][first, item].astype(F32)
            for q in range(1, nd):
                total = total + back_ins[r][first + q, item].astype(F32)
            parts.append(total)
        return parts[0] if ec == 1 else jnp.concatenate(parts)

    def rows_of(r, items):
        parts = [ins[r][:, i].astype(F32).reshape(group * CAP, model) for i in items]
        rows = parts[0] if len(parts) == 1 else jnp.concatenate(parts)
        return rows.astype(BF)

    def give(r, item, rows):
        back_outs[r][:, item] = rows.reshape(group, CAP, model).astype(BF)

    gr = group * CAP

    def half_forward(rows):
        return mm(rows, wg[...]), mm(rows, wu[...])

    def finish_forward(gp, up):
        return mm((gp * jax.nn.sigmoid(gp) * up).astype(BF), wd[...])

    def backward(rows, gp, up):
        act = mm_t(rows, wd[...])
        sig = jax.nn.sigmoid(gp)
        grad_gate = (act * up * sig * (1.0 + gp * (1.0 - sig))).astype(BF)
        grad_up = (act * gp * sig).astype(BF)
        return mm_t(grad_gate, wg[...]) + mm_t(grad_up, wu[...])

    names = ("fx1", "fx2", "k0a", "k0b", "k1a", "k1b", "d0a", "d0b", "d1a", "d1b", "g0", "g1")

    def at(name, st):
        return names.index(name) * 2 + st

    for st in range(2):
        f, b = st, 2 + st
        both = pick(0, f, state[f])
        vals[at("fx1", st)], vals[at("fx2", st)] = both[:width], both[width:]
        put(0, 0, f, False, unit_norm(both[:width], gain(f, False))[0])
        for slot in range(2):
            both = pick(slot, b, saved[slot, st])
            vals[at(f"k{slot}a", st)], vals[at(f"k{slot}b", st)] = both[:width], both[width:]
            put(0, 1 + slot, b, False, unit_norm(both[:width], gain(b, False))[0])
    send(0, True)
    for st in range(2):
        both = pick(0, 2 + st, state[2 + st])
        vals[at("d0a", st)], vals[at("d0b", st)] = both[:width], both[width:]
        put(1, 2, 2 + st, True, gate(0, 2 + st, True) * both[width:])
    for copy in weight_copies:
        copy.wait()
    receive(0, True)
    gp, up = half_forward(rows_of(0, (0, 1, 2)))
    for slot in range(2):
        pre[2 * slot] = gp[(1 + slot) * gr:(2 + slot) * gr]
        pre[2 * slot + 1] = up[(1 + slot) * gr:(2 + slot) * gr]
    rows = finish_forward(gp, up)
    for i in range(3):
        give(0, i, rows[i * gr:(i + 1) * gr])
    send(0, False)
    receive(0, False)

    def forward_middle(slot, st, r, item):
        add = gate(slot, st, False) * got(r, item, st, False)
        vals[at("fx1", st)] = vals[at("fx1", st)] + add
        middle = vals[at("fx2", st)] + mix(overlap(slot, st), add)
        vals[at("fx2", st)] = middle
        return unit_norm(middle, gain(st, True))[0]

    for st in range(2):
        put(1, 0, st, True, forward_middle(0, st, 0, 0))
        for slot in range(2):
            b = 2 + st
            add = gate(slot, b, False) * got(0, 1 + slot, b, False)
            middle = vals[at(f"k{slot}b", st)] + mix(overlap(slot, b), add)
            vals[at(f"k{slot}b", st)] = middle
            put(1, 1 if slot == 0 else 3, b, True, unit_norm(middle, gain(b, True))[0])
    send(1, True)
    receive(1, True)
    gp, up = half_forward(rows_of(1, (0, 1, 3)))
    pre[4], pre[5] = gp[2 * gr:], up[2 * gr:]
    give(1, 0, finish_forward(gp[:gr], up[:gr]))
    give(1, 1, backward(rows_of(1, (2,)), gp[gr:2 * gr], up[gr:2 * gr]))
    send(1, False)
    receive(1, False)

    def final_patch(slot, unit, first_rows, second_rows, last_second):
        a = unit % 2
        s1, s2 = sel[tab(slot, unit, a)], sel[tab(slot, unit, 1 - a)]
        if last_second:
            s1 = s1 * (1.0 - jnp.sum(s2, axis=0, keepdims=True))
        else:
            s2 = s2 * (1.0 - jnp.sum(s1, axis=0, keepdims=True))
        return (
            jnp.concatenate([first_rows, second_rows]).astype(BF),
            jnp.concatenate([s1, s2]).astype(BF),
        )

    def send_patch(unit, patch):
        patch_out[unit, :, :model] = patch[0]
        patch_out[unit, :, model:] = patch[1]
        start_if(patches[unit])

    def forward_end(slot, st, r, item):
        second = vals[at("fx2", st)] + gate(slot, st, True) * got(r, item, st, True)
        return final_patch(slot, st, vals[at("fx1", st)], second, True)

    def backward_middle(slot, st, r, item):
        b = 2 + st
        middle = vals[at(f"k{slot}b", st)]
        inv = unit_norm(middle, gain(b, True))[1]
        step = back_norm(middle, inv, gain(b, True), got(r, item, b, True))
        vals[at(f"d{slot}b", st)] = vals[at(f"d{slot}b", st)] + step
        inner = vals[at(f"d{slot}a", st)] + mix(overlap_t(slot, b), step)
        vals[at(f"d{slot}a", st)] = inner
        return gate(slot, b, False) * inner

    def backward_end(slot, st, r, item):
        b = 2 + st
        start = vals[at(f"k{slot}a", st)]
        inv = unit_norm(start, gain(b, False))[1]
        first = vals[at(f"d{slot}a", st)] + back_norm(start, inv, gain(b, False), got(r, item, b, False))
        return final_patch(slot, b, first, vals[at(f"d{slot}b", st)], False)

    for st in range(2):
        send_patch(st, forward_end(0, st, 1, 0))
    for st in range(2):
        put(2, 0, 2 + st, False, backward_middle(0, st, 1, 1))
    for st in range(2):
        wait_bulk(st)
        wait_patch(st)
        both = pick_new(st, patch_in[st])
        vals[at("fx1", st)], vals[at("fx2", st)] = both[:width], both[width:]
        put(2, 1, st, False, unit_norm(both[:width], gain(st, False))[0])
    send(2, True)
    receive(2, True)
    give(2, 0, backward(rows_of(2, (0,)), pre[0], pre[1]))
    gp, up = half_forward(rows_of(2, (1,)))
    give(2, 1, finish_forward(gp, up))
    send(2, False)
    receive(2, False)

    for st in range(2):
        send_patch(2 + st, backward_end(0, st, 2, 0))
    for st in range(2):
        put(3, 0, st, True, forward_middle(1, st, 2, 1))
    for st in range(2):
        u = 2 + st
        wait_bulk(u)
        wait_patch(u)
        both = pick_new(u, patch_in[u])
        vals[at("d1a", st)], vals[at("d1b", st)] = both[:width], both[width:]
        put(3, 1, u, True, gate(1, u, True) * both[width:])
    send(3, True)
    receive(3, True)
    gp, up = half_forward(rows_of(3, (0,)))
    give(3, 0, finish_forward(gp, up))
    give(3, 1, backward(rows_of(3, (1,)), pre[4], pre[5]))
    send(3, False)
    receive(3, False)

    def write(unit, patch):
        new_rows, new_sel = patch
        old = patch_in[unit]
        fresh = 1.0 - jnp.sum(new_sel.astype(F32), axis=0, keepdims=True)
        old_sel = old[:, model:].astype(F32) * fresh
        kept = eye * (fresh - jnp.sum(old_sel, axis=0, keepdims=True))
        spread = mm_t(eye.astype(BF), jnp.concatenate([old_sel.astype(BF), new_sel])).astype(BF)
        rows = jnp.concatenate([old[:, :model], new_rows])
        out[unit] = (mm(kept.astype(BF), base[unit]) + mm(spread, rows)).astype(BF)

    for st in range(2):
        put(4, 0, 2 + st, False, backward_middle(1, st, 3, 1))
    send(4, True)
    for st in range(2):
        write(st, forward_end(1, st, 3, 0))
    receive(4, True)
    give(4, 0, backward(rows_of(4, (0,)), pre[2], pre[3]))
    send(4, False)
    receive(4, False)
    for st in range(2):
        write(2 + st, backward_end(1, st, 4, 0))

    for r in range(5):
        drain(r, True)
        drain(r, False)
    for triple in bulk + patches:
        @pl.when(triple[0])
        def _(triple=triple):
            triple[2].wait_send()


def local(sizes, state_in, entering, saved, route_ids, gate_vals, w_gate, w_up, w_down, gains):
    ns, ne, nd = sizes
    group, width = ne * nd, ne // 2 * CAP
    units, tokens, model = state_in.shape[1:]
    hidden = w_gate.shape[-1]
    tables = route_ids.shape[1] * route_ids.shape[2] * route_ids.shape[3]
    topk = route_ids.shape[-1]
    ids = jnp.swapaxes(route_ids.reshape(tables, tokens, topk), 1, 2)
    gates = jnp.swapaxes(gate_vals.reshape(tables, tokens, topk), 1, 2)
    vmem = pl.BlockSpec(memory_space=pltpu.VMEM)
    anywhere = pl.BlockSpec(memory_space=pl.ANY)
    dma = pltpu.SemaphoreType.DMA
    scratch = (
        [pltpu.VMEM((ne, n, CAP, model), BF) for n in ITEMS_OUT]
        + [pltpu.VMEM((group, n, CAP, model), BF) for n in ITEMS_OUT]
        + [pltpu.VMEM((group, n, CAP, model), BF) for n in ITEMS_BACK]
        + [pltpu.VMEM((group, n, CAP, model), BF) for n in ITEMS_BACK]
        + [
            pltpu.VMEM((units, tokens, model), BF),
            pltpu.VMEM((units, 2 * width, model + tokens), BF),
            pltpu.VMEM((units, 2 * width, model + tokens), BF),
            pltpu.VMEM((tables, width, tokens), F32),
            pltpu.VMEM((tables, width, tokens), F32),
            pltpu.VMEM((24, width, model), F32),
            pltpu.VMEM((6, group * CAP, hidden), F32),
            pltpu.VMEM((model, hidden), BF),
            pltpu.VMEM((model, hidden), BF),
            pltpu.VMEM((hidden, model), BF),
            dma((10, group)), dma((10, group)), dma((10,)),
            dma((2, units)), dma((2, units)), dma((units,)), dma((3,)),
        ]
    )
    result = pl.pallas_call(
        functools.partial(kernel, sizes),
        out_shape=jax.ShapeDtypeStruct((units, tokens, model), BF),
        in_specs=[vmem, anywhere, vmem, vmem, vmem, anywhere, anywhere, anywhere, vmem],
        out_specs=vmem,
        scratch_shapes=scratch,
        compiler_params=pltpu.CompilerParams(
            collective_id=0, has_side_effects=True, vmem_limit_bytes=67043328
        ),
    )(state_in[0], entering[0], saved[0], ids, gates, w_gate[0, 0], w_up[0, 0], w_down[0, 0], gains[0])
    return result[None]


def solution(mesh):
    in_specs = (
        P("segment", None, ("expert", "dp"), None),
        P(None, None, ("expert", "dp"), None),
        P("segment", None, None, ("expert", "dp"), None),
        P("segment", None, None, None, ("expert", "dp"), None),
        P("segment", None, None, None, ("expert", "dp"), None),
        P("segment", "expert", None, "dp"),
        P("segment", "expert", None, "dp"),
        P("segment", "expert", "dp", None),
        P("segment", None, None),
    )
    out_specs = P("segment", None, ("expert", "dp"), None)
    sizes = (mesh.shape["segment"], mesh.shape["expert"], mesh.shape["dp"])
    body = functools.partial(local, sizes)
    return jax.shard_map(body, mesh=mesh, in_specs=in_specs, out_specs=out_specs, check_vma=False)
```

```python
import functools
import jax
import jax.numpy as jnp
from jax import lax
from jax.experimental import pallas as pl
from jax.experimental.pallas import tpu as pltpu
from jax.sharding import PartitionSpec as P

CAP = 8
EPSILON = 1e-06
LAST = (((1,), (1,)), ((), ()))
MESH = pl.DeviceIdType.MESH
BF = jnp.bfloat16
F32 = jnp.float32
ITEMS_OUT = (3, 4, 2, 2, 1)
ITEMS_BACK = (3, 2, 2, 2, 1)


def mm(a, b):
    return jnp.dot(a, b, preferred_element_type=F32)


def mm_t(a, b):
    return lax.dot_general(a, b, LAST, preferred_element_type=F32)


def mix(overlap, rows):
    picks = overlap.astype(BF)
    high = rows.astype(BF)
    rest = rows - high.astype(F32)
    mid = rest.astype(BF)
    low = (rest - mid.astype(F32)).astype(BF)
    return mm(picks, high) + (mm(picks, mid) + mm(picks, low))


def unit_norm(rows, gain):
    inv = lax.rsqrt(jnp.mean(rows * rows, axis=-1, keepdims=True) + EPSILON)
    return (rows * inv * gain).astype(BF), inv


def back_norm(rows, inv, gain, grad):
    weighted = gain * grad
    total = jnp.sum(weighted * rows, axis=-1, keepdims=True)
    return inv * weighted - rows * (inv * inv * inv) * total / rows.shape[-1]


def kernel(sizes, state_in, entering, saved_in, ids, gates, wg_in, wu_in, wd_in, gains, out, *scratch):
    ns, ne, nd = sizes
    group = ne * nd
    ec = ne // 2
    width = ec * CAP
    tokens, model = state_in.shape[1], state_in.shape[2]
    outs, ins, back_outs, back_ins = scratch[0:5], scratch[5:10], scratch[10:15], scratch[15:20]
    (base, patch_out, patch_in, sel, gate_col, vals, pre, wg, wu, wd,
     send_sem, recv_sem, local_sem, relay_send, relay_recv, enter_sem, weight_sem, state, saved, input_sem) = scratch[20:]
    seg, ex, dp = lax.axis_index("segment"), lax.axis_index("expert"), lax.axis_index("dp")
    me = ex * nd + dp

    input_copies = [
        pltpu.make_async_copy(state_in, state, input_sem.at[0]),
        pltpu.make_async_copy(saved_in, saved, input_sem.at[1]),
    ]
    for copy in input_copies:
        copy.start()
    weight_copies = [
        pltpu.make_async_copy(source, dest, weight_sem.at[i])
        for i, (source, dest) in enumerate(((wg_in, wg), (wu_in, wu), (wd_in, wd)))
    ]
    for copy in weight_copies:
        copy.start()

    barrier = pltpu.get_barrier_semaphore()

    @pl.loop(1, group)
    def _(k):
        t = lax.rem(me + k, group)
        pl.semaphore_signal(
            barrier, inc=1, device_id=(seg, lax.div(t, nd), lax.rem(t, nd)), device_id_type=MESH
        )

    has_up, has_down = seg < ns - 1, seg > 0

    @pl.when(has_up)
    def _():
        pl.semaphore_signal(barrier, inc=1, device_id=(seg + 1, ex, dp), device_id_type=MESH)

    @pl.when(has_down)
    def _():
        pl.semaphore_signal(barrier, inc=1, device_id=(seg - 1, ex, dp), device_id_type=MESH)

    lane = lax.broadcasted_iota(jnp.int32, (tokens, tokens), 1)
    row = lax.broadcasted_iota(jnp.int32, (tokens, tokens), 0)
    before = (row < lane).astype(F32).astype(BF)
    eye = (row == lane).astype(F32)
    slot_row = lax.broadcasted_iota(jnp.int32, (CAP, tokens), 0).astype(F32)
    for e in range(ec):
        match = ids[...] == e
        routed = jnp.sum(match.astype(F32), axis=1)
        weight = jnp.sum(jnp.where(match, gates[...], 0.0), axis=1)
        earlier = mm(routed.astype(BF), before)
        for tb in range(ids.shape[0]):
            hit = (routed[tb:tb + 1] == 1.0) & (earlier[tb:tb + 1] == slot_row)
            one = jnp.where(hit, 1.0, 0.0)
            sel[tb, e * CAP:(e + 1) * CAP] = one
            gate_col[tb, e * CAP:(e + 1) * CAP] = jnp.broadcast_to(
                jnp.sum(one * weight[tb:tb + 1], axis=1, keepdims=True), (CAP, tokens)
            )

    neighbours = jnp.where(has_up, 1, 0) + jnp.where(has_down, 1, 0)
    pl.semaphore_wait(barrier, group - 1 + neighbours)

    def relay(unit, kind, source, dest):
        up = unit in (0, 3)
        goes, comes = (has_up, has_down) if up else (has_down, has_up)
        target = lax.rem(seg + (1 if up else ns - 1), ns)
        copy = pltpu.make_async_remote_copy(
            src_ref=source, dst_ref=dest, send_sem=relay_send.at[kind, unit],
            recv_sem=relay_recv.at[kind, unit], device_id=(target, ex, dp), device_id_type=MESH,
        )
        return goes, comes, copy

    def start_if(triple):
        @pl.when(triple[0])
        def _():
            triple[2].start()

    bulk = [relay(u, 0, state_in.at[u], base.at[u]) for u in range(4)]
    enter = [pltpu.make_async_copy(entering.at[u], base.at[u], enter_sem.at[u]) for u in range(4)]
    for u in range(4):
        start_if(bulk[u])

        @pl.when(jnp.logical_not(bulk[u][1]))
        def _(u=u):
            enter[u].start()

    def wait_bulk(u):
        @pl.when(bulk[u][1])
        def _():
            bulk[u][2].wait_recv()

        @pl.when(jnp.logical_not(bulk[u][1]))
        def _():
            enter[u].wait()

    patches = [relay(u, 1, patch_out.at[u], patch_in.at[u]) for u in range(4)]
    for u in range(4):
        @pl.when(jnp.logical_not(patches[u][1]))
        def _(u=u):
            patch_in[u] = jnp.zeros(patch_in.shape[1:], BF)

    def wait_patch(u):
        @pl.when(patches[u][1])
        def _():
            patches[u][2].wait_recv()

    def peer(t):
        return (seg, lax.div(t, nd), lax.rem(t, nd))

    def phase_of(r, outward, item):
        return sum(ITEMS_OUT[:r]) + item if outward else sum(ITEMS_OUT) + sum(ITEMS_BACK[:r]) + item

    def step_copy(r, k, outward, item, target):
        if outward:
            source, dest = outs[r].at[lax.div(target, nd), item], ins[r].at[me, item]
        else:
            source, dest = back_outs[r].at[target, item], back_ins[r].at[me, item]
        phase = phase_of(r, outward, item)
        return pltpu.make_async_remote_copy(
            src_ref=source, dst_ref=dest, send_sem=send_sem.at[phase, k],
            recv_sem=recv_sem.at[phase, k], device_id=peer(target), device_id_type=MESH,
        )

    def own_copy(r, outward, item):
        source = outs[r].at[ex, item] if outward else back_outs[r].at[me, item]
        dest = ins[r].at[me, item] if outward else back_ins[r].at[me, item]
        return pltpu.make_async_copy(source, dest, local_sem.at[phase_of(r, outward, item)])

    def send(r, outward, item):
        @pl.loop(1, group)
        def _(k):
            step_copy(r, k, outward, item, lax.rem(me + k, group)).start()

        own_copy(r, outward, item).start()

    def receive(r, outward, *items):
        arrived = ins[r] if outward else back_ins[r]
        for item in items:
            phase = phase_of(r, outward, item)

            @pl.loop(1, group)
            def _(k, item=item, phase=phase):
                slot = arrived.at[lax.rem(me - k + group, group), item]
                pltpu.make_async_remote_copy(
                    src_ref=slot, dst_ref=slot, send_sem=send_sem.at[phase, k],
                    recv_sem=recv_sem.at[phase, k], device_id=peer(me), device_id_type=MESH,
                ).wait_recv()

            own_copy(r, outward, item).wait()

    def drain(r, outward, item):
        @pl.loop(1, group)
        def _(k):
            step_copy(r, k, outward, item, lax.rem(me + k, group)).wait_send()

    def tab(slot, unit, sub):
        return (slot * 4 + unit) * 2 + sub

    def pick(slot, unit, values):
        first = unit % 2
        both = jnp.concatenate([sel[tab(slot, unit, first)], sel[tab(slot, unit, 1 - first)]])
        return mm(both.astype(BF), values)

    def pick_new(unit, old):
        first = unit % 2
        both = jnp.concatenate([sel[tab(1, unit, first)], sel[tab(1, unit, 1 - first)]])
        held = old[:, model:]
        keep = 1.0 - jnp.sum(held.astype(F32), axis=0, keepdims=True)
        moved = mm_t(both.astype(BF), held).astype(BF)
        return mm((both * keep).astype(BF), base[unit]) + mm(moved, old[:, :model])

    def overlap(slot, unit):
        first = unit % 2
        return mm_t(sel[tab(slot, unit, 1 - first)].astype(BF), sel[tab(slot, unit, first)].astype(BF))

    def overlap_t(slot, unit):
        first = unit % 2
        return mm_t(sel[tab(slot, unit, first)].astype(BF), sel[tab(slot, unit, 1 - first)].astype(BF))

    def gate(slot, unit, second):
        sub = 1 - unit % 2 if second else unit % 2
        return gate_col[tab(slot, unit, sub)][:, 0:1]

    def gain(unit, second):
        sub = 1 - unit % 2 if second else unit % 2
        return gains[sub:sub + 1]

    def put(r, item, unit, second, rows):
        side = 1 - unit % 2 if second else unit % 2
        for e in range(ec):
            outs[r][side * ec + e, item] = rows[e * CAP:(e + 1) * CAP].astype(BF)

    def got(r, item, unit, second):
        side = 1 - unit % 2 if second else unit % 2
        parts = []
        for e in range(ec):
            first = (side * ec + e) * nd
            total = back_ins[r][first, item].astype(F32)
            for q in range(1, nd):
                total = total + back_ins[r][first + q, item].astype(F32)
            parts.append(total)
        return parts[0] if ec == 1 else jnp.concatenate(parts)

    def rows_of(r, items):
        parts = [ins[r][:, i].astype(F32).reshape(group * CAP, model) for i in items]
        rows = parts[0] if len(parts) == 1 else jnp.concatenate(parts)
        return rows.astype(BF)

    def give(r, item, rows):
        back_outs[r][:, item] = rows.reshape(group, CAP, model).astype(BF)

    gr = group * CAP

    def half_forward(rows):
        return mm(rows, wg[...]), mm(rows, wu[...])

    def finish_forward(gp, up):
        return mm((gp * jax.nn.sigmoid(gp) * up).astype(BF), wd[...])

    def backward(rows, gp, up):
        act = mm_t(rows, wd[...])
        sig = jax.nn.sigmoid(gp)
        grad_gate = (act * up * sig * (1.0 + gp * (1.0 - sig))).astype(BF)
        grad_up = (act * gp * sig).astype(BF)
        return mm_t(grad_gate, wg[...]) + mm_t(grad_up, wu[...])

    names = ("fx1", "fx2", "k0a", "k0b", "k1a", "k1b", "d0a", "d0b", "d1a", "d1b", "g0", "g1")

    def at(name, st):
        return names.index(name) * 2 + st

    def forward_middle(slot, st, r, item):
        add = gate(slot, st, False) * got(r, item, st, False)
        vals[at("fx1", st)] = vals[at("fx1", st)] + add
        middle = vals[at("fx2", st)] + mix(overlap(slot, st), add)
        vals[at("fx2", st)] = middle
        return unit_norm(middle, gain(st, True))[0]

    def final_patch(slot, unit, first_rows, second_rows, last_second):
        a = unit % 2
        s1, s2 = sel[tab(slot, unit, a)], sel[tab(slot, unit, 1 - a)]
        if last_second:
            s1 = s1 * (1.0 - jnp.sum(s2, axis=0, keepdims=True))
        else:
            s2 = s2 * (1.0 - jnp.sum(s1, axis=0, keepdims=True))
        return (
            jnp.concatenate([first_rows, second_rows]).astype(BF),
            jnp.concatenate([s1, s2]).astype(BF),
        )

    def send_patch(unit, patch):
        patch_out[unit, :, :model] = patch[0]
        patch_out[unit, :, model:] = patch[1]
        start_if(patches[unit])

    def forward_end(slot, st, r, item):
        second = vals[at("fx2", st)] + gate(slot, st, True) * got(r, item, st, True)
        return final_patch(slot, st, vals[at("fx1", st)], second, True)

    def backward_middle(slot, st, r, item):
        b = 2 + st
        middle = vals[at(f"k{slot}b", st)]
        inv = unit_norm(middle, gain(b, True))[1]
        step = back_norm(middle, inv, gain(b, True), got(r, item, b, True))
        vals[at(f"d{slot}b", st)] = vals[at(f"d{slot}b", st)] + step
        inner = vals[at(f"d{slot}a", st)] + mix(overlap_t(slot, b), step)
        vals[at(f"d{slot}a", st)] = inner
        return gate(slot, b, False) * inner

    def backward_end(slot, st, r, item):
        b = 2 + st
        start = vals[at(f"k{slot}a", st)]
        inv = unit_norm(start, gain(b, False))[1]
        first = vals[at(f"d{slot}a", st)] + back_norm(start, inv, gain(b, False), got(r, item, b, False))
        return final_patch(slot, b, first, vals[at(f"d{slot}b", st)], False)

    def write(unit, patch):
        new_rows, new_sel = patch
        old = patch_in[unit]
        fresh = 1.0 - jnp.sum(new_sel.astype(F32), axis=0, keepdims=True)
        old_sel = old[:, model:].astype(F32) * fresh
        kept = eye * (fresh - jnp.sum(old_sel, axis=0, keepdims=True))
        spread = mm_t(eye.astype(BF), jnp.concatenate([old_sel.astype(BF), new_sel])).astype(BF)
        rows = jnp.concatenate([old[:, :model], new_rows])
        out[unit] = (mm(kept.astype(BF), base[unit]) + mm(spread, rows)).astype(BF)

    both_streams = range(2)

    def start_kept(slot, item):
        for st in both_streams:
            b = 2 + st
            both = pick(slot, b, saved[slot, st])
            vals[at(f"k{slot}a", st)], vals[at(f"k{slot}b", st)] = both[:width], both[width:]
            put(0, item, b, False, unit_norm(both[:width], gain(b, False))[0])
        send(0, True, item)

    def middle_kept(slot, item, to):
        receive(0, False, item)
        for st in both_streams:
            b = 2 + st
            add = gate(slot, b, False) * got(0, item, b, False)
            middle = vals[at(f"k{slot}b", st)] + mix(overlap(slot, b), add)
            vals[at(f"k{slot}b", st)] = middle
            put(1, to, b, True, unit_norm(middle, gain(b, True))[0])
        send(1, True, to)

    input_copies[0].wait()
    for st in both_streams:
        both = pick(0, st, state[st])
        vals[at("fx1", st)], vals[at("fx2", st)] = both[:width], both[width:]
        put(0, 0, st, False, unit_norm(both[:width], gain(st, False))[0])
    send(0, True, 0)
    input_copies[1].wait()
    start_kept(0, 1)
    for st in both_streams:
        both = pick(0, 2 + st, state[2 + st])
        vals[at("d0a", st)], vals[at("d0b", st)] = both[:width], both[width:]
        put(1, 2, 2 + st, True, gate(0, 2 + st, True) * both[width:])
    send(1, True, 2)
    for copy in weight_copies:
        copy.wait()
    receive(0, True, 0)
    gp, up = half_forward(rows_of(0, (0,)))
    give(0, 0, finish_forward(gp, up))
    send(0, False, 0)
    receive(0, True, 1)
    gp, up = half_forward(rows_of(0, (1,)))
    pre[0], pre[1] = gp, up
    give(0, 1, finish_forward(gp, up))
    send(0, False, 1)
    start_kept(1, 2)
    receive(0, False, 0)
    for st in both_streams:
        put(1, 0, st, True, forward_middle(0, st, 0, 0))
    send(1, True, 0)
    middle_kept(0, 1, 1)
    receive(0, True, 2)
    gp, up = half_forward(rows_of(0, (2,)))
    pre[2], pre[3] = gp, up
    give(0, 2, finish_forward(gp, up))
    send(0, False, 2)

    receive(1, True, 0)
    give(1, 0, finish_forward(*half_forward(rows_of(1, (0,)))))
    send(1, False, 0)
    receive(1, True, 1, 2)
    gp, up = half_forward(rows_of(1, (1,)))
    give(1, 1, backward(rows_of(1, (2,)), gp, up))
    send(1, False, 1)
    receive(1, False, 0)
    for st in both_streams:
        send_patch(st, forward_end(0, st, 1, 0))
    middle_kept(1, 2, 3)
    receive(1, False, 1)
    for st in both_streams:
        put(2, 0, 2 + st, False, backward_middle(0, st, 1, 1))
    send(2, True, 0)

    for st in both_streams:
        wait_bulk(st)
        wait_patch(st)
        both = pick_new(st, patch_in[st])
        vals[at("fx1", st)], vals[at("fx2", st)] = both[:width], both[width:]
        put(2, 1, st, False, unit_norm(both[:width], gain(st, False))[0])
    send(2, True, 1)
    receive(2, True, 0)
    give(2, 0, backward(rows_of(2, (0,)), pre[0], pre[1]))
    send(2, False, 0)
    receive(2, True, 1)
    give(2, 1, finish_forward(*half_forward(rows_of(2, (1,)))))
    send(2, False, 1)
    receive(1, True, 3)
    pre[4], pre[5] = half_forward(rows_of(1, (3,)))
    receive(2, False, 0)
    for st in both_streams:
        send_patch(2 + st, backward_end(0, st, 2, 0))
    receive(2, False, 1)
    for st in both_streams:
        put(3, 0, st, True, forward_middle(1, st, 2, 1))

    for st in both_streams:
        u = 2 + st
        wait_bulk(u)
        wait_patch(u)
        both = pick_new(u, patch_in[u])
        vals[at("d1a", st)], vals[at("d1b", st)] = both[:width], both[width:]
        put(3, 1, u, True, gate(1, u, True) * both[width:])
    send(3, True, 1)
    send(3, True, 0)
    receive(3, True, 1)
    give(3, 1, backward(rows_of(3, (1,)), pre[4], pre[5]))
    send(3, False, 1)
    receive(3, True, 0)
    give(3, 0, finish_forward(*half_forward(rows_of(3, (0,)))))
    send(3, False, 0)
    receive(3, False, 1)
    for st in both_streams:
        put(4, 0, 2 + st, False, backward_middle(1, st, 3, 1))
    send(4, True, 0)
    receive(3, False, 0)
    for st in both_streams:
        write(st, forward_end(1, st, 3, 0))
    receive(4, True, 0)
    give(4, 0, backward(rows_of(4, (0,)), pre[2], pre[3]))
    send(4, False, 0)
    receive(4, False, 0)
    for st in both_streams:
        write(2 + st, backward_end(1, st, 4, 0))

    for r in range(5):
        for item in range(ITEMS_OUT[r]):
            drain(r, True, item)
        for item in range(ITEMS_BACK[r]):
            drain(r, False, item)
    for triple in bulk + patches:
        @pl.when(triple[0])
        def _(triple=triple):
            triple[2].wait_send()


def local(sizes, state_in, entering, saved, route_ids, gate_vals, w_gate, w_up, w_down, gains):
    ns, ne, nd = sizes
    group, width = ne * nd, ne // 2 * CAP
    units, tokens, model = state_in.shape[1:]
    hidden = w_gate.shape[-1]
    tables = route_ids.shape[1] * route_ids.shape[2] * route_ids.shape[3]
    topk = route_ids.shape[-1]
    ids = jnp.swapaxes(route_ids.reshape(tables, tokens, topk), 1, 2)
    gates = jnp.swapaxes(gate_vals.reshape(tables, tokens, topk), 1, 2)
    vmem = pl.BlockSpec(memory_space=pltpu.VMEM)
    anywhere = pl.BlockSpec(memory_space=pl.ANY)
    dma = pltpu.SemaphoreType.DMA
    scratch = (
        [pltpu.VMEM((ne, n, CAP, model), BF) for n in ITEMS_OUT]
        + [pltpu.VMEM((group, n, CAP, model), BF) for n in ITEMS_OUT]
        + [pltpu.VMEM((group, n, CAP, model), BF) for n in ITEMS_BACK]
        + [pltpu.VMEM((group, n, CAP, model), BF) for n in ITEMS_BACK]
        + [
            pltpu.VMEM((units, tokens, model), BF),
            pltpu.VMEM((units, 2 * width, model + tokens), BF),
            pltpu.VMEM((units, 2 * width, model + tokens), BF),
            pltpu.VMEM((tables, width, tokens), F32),
            pltpu.VMEM((tables, width, tokens), F32),
            pltpu.VMEM((24, width, model), F32),
            pltpu.VMEM((6, group * CAP, hidden), F32),
            pltpu.VMEM((model, hidden), BF),
            pltpu.VMEM((model, hidden), BF),
            pltpu.VMEM((hidden, model), BF),
            dma((22, group)), dma((22, group)), dma((22,)),
            dma((2, units)), dma((2, units)), dma((units,)), dma((3,)),
            pltpu.VMEM((units, tokens, model), BF),
            pltpu.VMEM(saved.shape[1:], BF),
            dma((2,)),
        ]
    )
    result = pl.pallas_call(
        functools.partial(kernel, sizes),
        out_shape=jax.ShapeDtypeStruct((units, tokens, model), BF),
        in_specs=[anywhere, anywhere, anywhere, vmem, vmem, anywhere, anywhere, anywhere, vmem],
        out_specs=vmem,
        scratch_shapes=scratch,
        compiler_params=pltpu.CompilerParams(
            collective_id=0, has_side_effects=True, vmem_limit_bytes=67043328
        ),
    )(state_in[0], entering[0], saved[0], ids, gates, w_gate[0, 0], w_up[0, 0], w_down[0, 0], gains[0])
    return result[None]


def solution(mesh):
    in_specs = (
        P("segment", None, ("expert", "dp"), None),
        P(None, None, ("expert", "dp"), None),
        P("segment", None, None, ("expert", "dp"), None),
        P("segment", None, None, None, ("expert", "dp"), None),
        P("segment", None, None, None, ("expert", "dp"), None),
        P("segment", "expert", None, "dp"),
        P("segment", "expert", None, "dp"),
        P("segment", "expert", "dp", None),
        P("segment", None, None),
    )
    out_specs = P("segment", None, ("expert", "dp"), None)
    sizes = (mesh.shape["segment"], mesh.shape["expert"], mesh.shape["dp"])
    body = functools.partial(local, sizes)
    return jax.shard_map(body, mesh=mesh, in_specs=in_specs, out_specs=out_specs, check_vma=False)
```

```python
import functools
import jax
import jax.numpy as jnp
from jax import lax
from jax.experimental import pallas as pl
from jax.experimental.pallas import tpu as pltpu
from jax.sharding import PartitionSpec as P

CAP = 8
EPSILON = 1e-06
LAST = (((1,), (1,)), ((), ()))
MESH = pl.DeviceIdType.MESH
BF = jnp.bfloat16
F32 = jnp.float32
ITEMS_OUT = (3, 4, 2, 2, 1)
ITEMS_BACK = (3, 2, 2, 2, 1)


def mm(a, b):
    return jnp.dot(a, b, preferred_element_type=F32)


def mm_t(a, b):
    return lax.dot_general(a, b, LAST, preferred_element_type=F32)


def mix(overlap, rows):
    picks = overlap.astype(BF)
    high = rows.astype(BF)
    rest = rows - high.astype(F32)
    mid = rest.astype(BF)
    low = (rest - mid.astype(F32)).astype(BF)
    return mm(picks, high) + (mm(picks, mid) + mm(picks, low))


def unit_norm(rows, gain):
    inv = lax.rsqrt(jnp.mean(rows * rows, axis=-1, keepdims=True) + EPSILON)
    return (rows * inv * gain).astype(BF), inv


def back_norm(rows, inv, gain, grad):
    weighted = gain * grad
    total = jnp.sum(weighted * rows, axis=-1, keepdims=True)
    return inv * weighted - rows * (inv * inv * inv) * total / rows.shape[-1]


def kernel(sizes, state_in, entering, saved_in, ids, gates, wg_in, wu_in, wd_in, gains, out, *scratch):
    ns, ne, nd = sizes
    group = ne * nd
    ec = ne // 2
    width = ec * CAP
    tokens, model = state_in.shape[1], state_in.shape[2]
    outs, ins, back_outs, back_ins = scratch[0:5], scratch[5:10], scratch[10:15], scratch[15:20]
    (base, patch_out, patch_in, sel, gate_col, vals, pre, wg, wu, wd,
     send_sem, recv_sem, local_sem, relay_send, relay_recv, enter_sem, weight_sem, state, saved, input_sem) = scratch[20:]
    seg, ex, dp = lax.axis_index("segment"), lax.axis_index("expert"), lax.axis_index("dp")
    me = ex * nd + dp

    input_copies = [
        pltpu.make_async_copy(state_in, state, input_sem.at[0]),
        pltpu.make_async_copy(saved_in, saved, input_sem.at[1]),
    ]
    for copy in input_copies:
        copy.start()
    weight_copies = [
        pltpu.make_async_copy(source, dest, weight_sem.at[i])
        for i, (source, dest) in enumerate(((wg_in, wg), (wu_in, wu), (wd_in, wd)))
    ]
    for copy in weight_copies:
        copy.start()

    barrier = pltpu.get_barrier_semaphore()

    @pl.loop(1, group)
    def _(k):
        t = lax.rem(me + k, group)
        pl.semaphore_signal(
            barrier, inc=1, device_id=(seg, lax.div(t, nd), lax.rem(t, nd)), device_id_type=MESH
        )

    has_up, has_down = seg < ns - 1, seg > 0

    @pl.when(has_up)
    def _():
        pl.semaphore_signal(barrier, inc=1, device_id=(seg + 1, ex, dp), device_id_type=MESH)

    @pl.when(has_down)
    def _():
        pl.semaphore_signal(barrier, inc=1, device_id=(seg - 1, ex, dp), device_id_type=MESH)

    lane = lax.broadcasted_iota(jnp.int32, (tokens, tokens), 1)
    row = lax.broadcasted_iota(jnp.int32, (tokens, tokens), 0)
    before = (row < lane).astype(F32).astype(BF)
    eye = (row == lane).astype(F32)
    slot_row = lax.broadcasted_iota(jnp.int32, (CAP, tokens), 0).astype(F32)
    for e in range(ec):
        match = ids[...] == e
        routed = jnp.sum(match.astype(F32), axis=1)
        weight = jnp.sum(jnp.where(match, gates[...], 0.0), axis=1)
        earlier = mm(routed.astype(BF), before)
        for tb in range(ids.shape[0]):
            hit = (routed[tb:tb + 1] == 1.0) & (earlier[tb:tb + 1] == slot_row)
            one = jnp.where(hit, 1.0, 0.0)
            sel[tb, e * CAP:(e + 1) * CAP] = one
            gate_col[tb, e * CAP:(e + 1) * CAP] = jnp.broadcast_to(
                jnp.sum(one * weight[tb:tb + 1], axis=1, keepdims=True), (CAP, tokens)
            )

    neighbours = jnp.where(has_up, 1, 0) + jnp.where(has_down, 1, 0)
    pl.semaphore_wait(barrier, group - 1 + neighbours)

    def relay(unit, kind, source, dest):
        up = unit in (0, 3)
        goes, comes = (has_up, has_down) if up else (has_down, has_up)
        target = lax.rem(seg + (1 if up else ns - 1), ns)
        copy = pltpu.make_async_remote_copy(
            src_ref=source, dst_ref=dest, send_sem=relay_send.at[kind, unit],
            recv_sem=relay_recv.at[kind, unit], device_id=(target, ex, dp), device_id_type=MESH,
        )
        return goes, comes, copy

    def start_if(triple):
        @pl.when(triple[0])
        def _():
            triple[2].start()

    bulk = [relay(u, 0, state_in.at[u], base.at[u]) for u in range(4)]
    enter = [pltpu.make_async_copy(entering.at[u], base.at[u], enter_sem.at[u]) for u in range(4)]
    for u in range(4):
        start_if(bulk[u])

        @pl.when(jnp.logical_not(bulk[u][1]))
        def _(u=u):
            enter[u].start()

    def wait_bulk(u):
        @pl.when(bulk[u][1])
        def _():
            bulk[u][2].wait_recv()

        @pl.when(jnp.logical_not(bulk[u][1]))
        def _():
            enter[u].wait()

    patches = [relay(u, 1, patch_out.at[u], patch_in.at[u]) for u in range(4)]
    for u in range(4):
        @pl.when(jnp.logical_not(patches[u][1]))
        def _(u=u):
            patch_in[u] = jnp.zeros(patch_in.shape[1:], BF)

    def wait_patch(u):
        @pl.when(patches[u][1])
        def _():
            patches[u][2].wait_recv()

    def peer(t):
        return (seg, lax.div(t, nd), lax.rem(t, nd))

    def phase_of(r, outward, item):
        return sum(ITEMS_OUT[:r]) + item if outward else sum(ITEMS_OUT) + sum(ITEMS_BACK[:r]) + item

    def step_copy(r, k, outward, item, target):
        if outward:
            source, dest = outs[r].at[lax.div(target, nd), item], ins[r].at[me, item]
        else:
            source, dest = back_outs[r].at[target, item], back_ins[r].at[me, item]
        phase = phase_of(r, outward, item)
        return pltpu.make_async_remote_copy(
            src_ref=source, dst_ref=dest, send_sem=send_sem.at[phase, k],
            recv_sem=recv_sem.at[phase, k], device_id=peer(target), device_id_type=MESH,
        )

    def own_copy(r, outward, item):
        source = outs[r].at[ex, item] if outward else back_outs[r].at[me, item]
        dest = ins[r].at[me, item] if outward else back_ins[r].at[me, item]
        return pltpu.make_async_copy(source, dest, local_sem.at[phase_of(r, outward, item)])

    def send(r, outward, item):
        @pl.loop(1, group)
        def _(k):
            step_copy(r, k, outward, item, lax.rem(me + k, group)).start()

        own_copy(r, outward, item).start()

    def receive(r, outward, *items):
        arrived = ins[r] if outward else back_ins[r]
        for item in items:
            phase = phase_of(r, outward, item)

            @pl.loop(1, group)
            def _(k, item=item, phase=phase):
                slot = arrived.at[lax.rem(me - k + group, group), item]
                pltpu.make_async_remote_copy(
                    src_ref=slot, dst_ref=slot, send_sem=send_sem.at[phase, k],
                    recv_sem=recv_sem.at[phase, k], device_id=peer(me), device_id_type=MESH,
                ).wait_recv()

            own_copy(r, outward, item).wait()

    def drain(r, outward, item):
        @pl.loop(1, group)
        def _(k):
            step_copy(r, k, outward, item, lax.rem(me + k, group)).wait_send()

    def tab(slot, unit, sub):
        return (slot * 4 + unit) * 2 + sub

    def pick(slot, unit, values):
        first = unit % 2
        both = jnp.concatenate([sel[tab(slot, unit, first)], sel[tab(slot, unit, 1 - first)]])
        return mm(both.astype(BF), values)

    def pick_new(unit, old):
        first = unit % 2
        both = jnp.concatenate([sel[tab(1, unit, first)], sel[tab(1, unit, 1 - first)]])
        held = old[:, model:]
        keep = 1.0 - jnp.sum(held.astype(F32), axis=0, keepdims=True)
        moved = mm_t(both.astype(BF), held).astype(BF)
        return mm((both * keep).astype(BF), base[unit]) + mm(moved, old[:, :model])

    def overlap(slot, unit):
        first = unit % 2
        return mm_t(sel[tab(slot, unit, 1 - first)].astype(BF), sel[tab(slot, unit, first)].astype(BF))

    def overlap_t(slot, unit):
        first = unit % 2
        return mm_t(sel[tab(slot, unit, first)].astype(BF), sel[tab(slot, unit, 1 - first)].astype(BF))

    def gate(slot, unit, second):
        sub = 1 - unit % 2 if second else unit % 2
        return gate_col[tab(slot, unit, sub)][:, 0:1]

    def gain(unit, second):
        sub = 1 - unit % 2 if second else unit % 2
        return gains[sub:sub + 1]

    def put(r, item, unit, second, rows):
        side = 1 - unit % 2 if second else unit % 2
        for e in range(ec):
            outs[r][side * ec + e, item] = rows[e * CAP:(e + 1) * CAP].astype(BF)

    def got(r, item, unit, second):
        side = 1 - unit % 2 if second else unit % 2
        parts = []
        for e in range(ec):
            first = (side * ec + e) * nd
            total = back_ins[r][first, item].astype(F32)
            for q in range(1, nd):
                total = total + back_ins[r][first + q, item].astype(F32)
            parts.append(total)
        return parts[0] if ec == 1 else jnp.concatenate(parts)

    def rows_of(r, items):
        parts = [ins[r][:, i].astype(F32).reshape(group * CAP, model) for i in items]
        rows = parts[0] if len(parts) == 1 else jnp.concatenate(parts)
        return rows.astype(BF)

    def give(r, item, rows):
        back_outs[r][:, item] = rows.reshape(group, CAP, model).astype(BF)

    gr = group * CAP

    def half_forward(rows):
        return mm(rows, wg[...]), mm(rows, wu[...])

    def finish_forward(gp, up):
        return mm((gp * jax.nn.sigmoid(gp) * up).astype(BF), wd[...])

    def backward(rows, gp, up):
        act = mm_t(rows, wd[...])
        sig = jax.nn.sigmoid(gp)
        grad_gate = (act * up * sig * (1.0 + gp * (1.0 - sig))).astype(BF)
        grad_up = (act * gp * sig).astype(BF)
        return mm_t(grad_gate, wg[...]) + mm_t(grad_up, wu[...])

    names = ("fx1", "fx2", "k0a", "k0b", "k1a", "k1b", "d0a", "d0b", "d1a", "d1b", "g0", "g1")

    def at(name, st):
        return names.index(name) * 2 + st

    def forward_middle(slot, st, r, item):
        add = gate(slot, st, False) * got(r, item, st, False)
        vals[at("fx1", st)] = vals[at("fx1", st)] + add
        middle = vals[at("fx2", st)] + mix(overlap(slot, st), add)
        vals[at("fx2", st)] = middle
        return unit_norm(middle, gain(st, True))[0]

    def final_patch(slot, unit, first_rows, second_rows, last_second):
        a = unit % 2
        s1, s2 = sel[tab(slot, unit, a)], sel[tab(slot, unit, 1 - a)]
        if last_second:
            s1 = s1 * (1.0 - jnp.sum(s2, axis=0, keepdims=True))
        else:
            s2 = s2 * (1.0 - jnp.sum(s1, axis=0, keepdims=True))
        return (
            jnp.concatenate([first_rows, second_rows]).astype(BF),
            jnp.concatenate([s1, s2]).astype(BF),
        )

    def send_patch(unit, patch):
        patch_out[unit, :, :model] = patch[0]
        patch_out[unit, :, model:] = patch[1]
        start_if(patches[unit])

    def forward_end(slot, st, r, item):
        second = vals[at("fx2", st)] + gate(slot, st, True) * got(r, item, st, True)
        return final_patch(slot, st, vals[at("fx1", st)], second, True)

    def backward_middle(slot, st, r, item):
        b = 2 + st
        middle = vals[at(f"k{slot}b", st)]
        inv = unit_norm(middle, gain(b, True))[1]
        step = back_norm(middle, inv, gain(b, True), got(r, item, b, True))
        vals[at(f"d{slot}b", st)] = vals[at(f"d{slot}b", st)] + step
        inner = vals[at(f"d{slot}a", st)] + mix(overlap_t(slot, b), step)
        vals[at(f"d{slot}a", st)] = inner
        return gate(slot, b, False) * inner

    def backward_end(slot, st, r, item):
        b = 2 + st
        start = vals[at(f"k{slot}a", st)]
        inv = unit_norm(start, gain(b, False))[1]
        first = vals[at(f"d{slot}a", st)] + back_norm(start, inv, gain(b, False), got(r, item, b, False))
        return final_patch(slot, b, first, vals[at(f"d{slot}b", st)], False)

    def write(unit, patch):
        new_rows, new_sel = patch
        old = patch_in[unit]
        fresh = 1.0 - jnp.sum(new_sel.astype(F32), axis=0, keepdims=True)
        old_sel = old[:, model:].astype(F32) * fresh
        kept = eye * (fresh - jnp.sum(old_sel, axis=0, keepdims=True))
        spread = mm_t(eye.astype(BF), jnp.concatenate([old_sel.astype(BF), new_sel])).astype(BF)
        rows = jnp.concatenate([old[:, :model], new_rows])
        out[unit] = (mm(kept.astype(BF), base[unit]) + mm(spread, rows)).astype(BF)

    both_streams = range(2)

    def start_kept(slot, item):
        for st in both_streams:
            b = 2 + st
            both = pick(slot, b, saved[slot, st])
            vals[at(f"k{slot}a", st)], vals[at(f"k{slot}b", st)] = both[:width], both[width:]
            put(0, item, b, False, unit_norm(both[:width], gain(b, False))[0])
        send(0, True, item)

    def middle_kept(slot, item, to):
        receive(0, False, item)
        for st in both_streams:
            b = 2 + st
            add = gate(slot, b, False) * got(0, item, b, False)
            middle = vals[at(f"k{slot}b", st)] + mix(overlap(slot, b), add)
            vals[at(f"k{slot}b", st)] = middle
            put(1, to, b, True, unit_norm(middle, gain(b, True))[0])
        send(1, True, to)

    input_copies[0].wait()
    for st in both_streams:
        both = pick(0, st, state[st])
        vals[at("fx1", st)], vals[at("fx2", st)] = both[:width], both[width:]
        put(0, 0, st, False, unit_norm(both[:width], gain(st, False))[0])
    send(0, True, 0)
    input_copies[1].wait()
    start_kept(0, 1)
    for st in both_streams:
        both = pick(0, 2 + st, state[2 + st])
        vals[at("d0a", st)], vals[at("d0b", st)] = both[:width], both[width:]
        put(1, 2, 2 + st, True, gate(0, 2 + st, True) * both[width:])
    send(1, True, 2)
    for copy in weight_copies:
        copy.wait()
    receive(0, True, 0)
    gp, up = half_forward(rows_of(0, (0,)))
    give(0, 0, finish_forward(gp, up))
    send(0, False, 0)
    receive(0, True, 1)
    gp, up = half_forward(rows_of(0, (1,)))
    pre[0], pre[1] = gp, up
    give(0, 1, finish_forward(gp, up))
    send(0, False, 1)
    receive(0, False, 0)
    for st in both_streams:
        put(1, 0, st, True, forward_middle(0, st, 0, 0))
    send(1, True, 0)
    middle_kept(0, 1, 1)
    start_kept(1, 2)

    receive(1, True, 0)
    give(1, 0, finish_forward(*half_forward(rows_of(1, (0,)))))
    send(1, False, 0)
    receive(1, True, 1, 2)
    gp, up = half_forward(rows_of(1, (1,)))
    give(1, 1, backward(rows_of(1, (2,)), gp, up))
    send(1, False, 1)
    receive(0, True, 2)
    gp, up = half_forward(rows_of(0, (2,)))
    pre[2], pre[3] = gp, up
    give(0, 2, finish_forward(gp, up))
    send(0, False, 2)
    receive(1, False, 0)
    for st in both_streams:
        send_patch(st, forward_end(0, st, 1, 0))
    receive(1, False, 1)
    for st in both_streams:
        put(2, 0, 2 + st, False, backward_middle(0, st, 1, 1))
    send(2, True, 0)

    for st in both_streams:
        wait_bulk(st)
        wait_patch(st)
        both = pick_new(st, patch_in[st])
        vals[at("fx1", st)], vals[at("fx2", st)] = both[:width], both[width:]
        put(2, 1, st, False, unit_norm(both[:width], gain(st, False))[0])
    send(2, True, 1)
    middle_kept(1, 2, 3)
    receive(2, True, 0)
    give(2, 0, backward(rows_of(2, (0,)), pre[0], pre[1]))
    send(2, False, 0)
    receive(2, True, 1)
    give(2, 1, finish_forward(*half_forward(rows_of(2, (1,)))))
    send(2, False, 1)
    receive(1, True, 3)
    pre[4], pre[5] = half_forward(rows_of(1, (3,)))
    receive(2, False, 0)
    for st in both_streams:
        send_patch(2 + st, backward_end(0, st, 2, 0))
    receive(2, False, 1)
    for st in both_streams:
        put(3, 0, st, True, forward_middle(1, st, 2, 1))

    for st in both_streams:
        u = 2 + st
        wait_bulk(u)
        wait_patch(u)
        both = pick_new(u, patch_in[u])
        vals[at("d1a", st)], vals[at("d1b", st)] = both[:width], both[width:]
        put(3, 1, u, True, gate(1, u, True) * both[width:])
    send(3, True, 1)
    send(3, True, 0)
    receive(3, True, 1)
    give(3, 1, backward(rows_of(3, (1,)), pre[4], pre[5]))
    send(3, False, 1)
    receive(3, True, 0)
    give(3, 0, finish_forward(*half_forward(rows_of(3, (0,)))))
    send(3, False, 0)
    receive(3, False, 1)
    for st in both_streams:
        put(4, 0, 2 + st, False, backward_middle(1, st, 3, 1))
    send(4, True, 0)
    receive(3, False, 0)
    for st in both_streams:
        write(st, forward_end(1, st, 3, 0))
    receive(4, True, 0)
    give(4, 0, backward(rows_of(4, (0,)), pre[2], pre[3]))
    send(4, False, 0)
    receive(4, False, 0)
    for st in both_streams:
        write(2 + st, backward_end(1, st, 4, 0))

    for r in range(5):
        for item in range(ITEMS_OUT[r]):
            drain(r, True, item)
        for item in range(ITEMS_BACK[r]):
            drain(r, False, item)
    for triple in bulk + patches:
        @pl.when(triple[0])
        def _(triple=triple):
            triple[2].wait_send()


def local(sizes, state_in, entering, saved, route_ids, gate_vals, w_gate, w_up, w_down, gains):
    ns, ne, nd = sizes
    group, width = ne * nd, ne // 2 * CAP
    units, tokens, model = state_in.shape[1:]
    hidden = w_gate.shape[-1]
    tables = route_ids.shape[1] * route_ids.shape[2] * route_ids.shape[3]
    topk = route_ids.shape[-1]
    ids = jnp.swapaxes(route_ids.reshape(tables, tokens, topk), 1, 2)
    gates = jnp.swapaxes(gate_vals.reshape(tables, tokens, topk), 1, 2)
    vmem = pl.BlockSpec(memory_space=pltpu.VMEM)
    anywhere = pl.BlockSpec(memory_space=pl.ANY)
    dma = pltpu.SemaphoreType.DMA
    scratch = (
        [pltpu.VMEM((ne, n, CAP, model), BF) for n in ITEMS_OUT]
        + [pltpu.VMEM((group, n, CAP, model), BF) for n in ITEMS_OUT]
        + [pltpu.VMEM((group, n, CAP, model), BF) for n in ITEMS_BACK]
        + [pltpu.VMEM((group, n, CAP, model), BF) for n in ITEMS_BACK]
        + [
            pltpu.VMEM((units, tokens, model), BF),
            pltpu.VMEM((units, 2 * width, model + tokens), BF),
            pltpu.VMEM((units, 2 * width, model + tokens), BF),
            pltpu.VMEM((tables, width, tokens), F32),
            pltpu.VMEM((tables, width, tokens), F32),
            pltpu.VMEM((24, width, model), F32),
            pltpu.VMEM((6, group * CAP, hidden), F32),
            pltpu.VMEM((model, hidden), BF),
            pltpu.VMEM((model, hidden), BF),
            pltpu.VMEM((hidden, model), BF),
            dma((22, group)), dma((22, group)), dma((22,)),
            dma((2, units)), dma((2, units)), dma((units,)), dma((3,)),
            pltpu.VMEM((units, tokens, model), BF),
            pltpu.VMEM(saved.shape[1:], BF),
            dma((2,)),
        ]
    )
    result = pl.pallas_call(
        functools.partial(kernel, sizes),
        out_shape=jax.ShapeDtypeStruct((units, tokens, model), BF),
        in_specs=[anywhere, anywhere, anywhere, vmem, vmem, anywhere, anywhere, anywhere, vmem],
        out_specs=vmem,
        scratch_shapes=scratch,
        compiler_params=pltpu.CompilerParams(
            collective_id=0, has_side_effects=True, vmem_limit_bytes=67043328
        ),
    )(state_in[0], entering[0], saved[0], ids, gates, w_gate[0, 0], w_up[0, 0], w_down[0, 0], gains[0])
    return result[None]


def solution(mesh):
    in_specs = (
        P("segment", None, ("expert", "dp"), None),
        P(None, None, ("expert", "dp"), None),
        P("segment", None, None, ("expert", "dp"), None),
        P("segment", None, None, None, ("expert", "dp"), None),
        P("segment", None, None, None, ("expert", "dp"), None),
        P("segment", "expert", None, "dp"),
        P("segment", "expert", None, "dp"),
        P("segment", "expert", "dp", None),
        P("segment", None, None),
    )
    out_specs = P("segment", None, ("expert", "dp"), None)
    sizes = (mesh.shape["segment"], mesh.shape["expert"], mesh.shape["dp"])
    body = functools.partial(local, sizes)
    return jax.shard_map(body, mesh=mesh, in_specs=in_specs, out_specs=out_specs, check_vma=False)
```
